32 devices in a mesh: grp: 2 (over y), dp: 4 (over z), tensor: 4 (over x, core).
Axes of the slice: x: 2, y: 2, z: 4, core: 2. Of those that a mesh axis runs over, the one named last changes fastest.
Arguments:
- x_train: bfloat16 [1024, 28672], P(('grp', 'dp'), 'tensor'), parts along dimension 0, may hold values from -6 to 6
- gout_train: bfloat16 [1024, 8192], P(('grp', 'dp'), 'tensor'), parts along dimension 0, may hold values from -6 to 6
- x_query: bfloat16 [256, 28672], P(('grp', 'dp'), 'tensor'), parts along dimension 0, may hold values from -6 to 6
- gout_query: bfloat16 [256, 8192], P(('grp', 'dp'), 'tensor'), parts along dimension 0, may hold values from -6 to 6
- proj_in: bfloat16 [28672, 64], P('tensor'), may hold values from -0.03125 to 0.03125
- proj_out: bfloat16 [8192, 32], P('tensor'), may hold values from -0.0625 to 0.0625
- train_lengths: int32 [64], P(('grp', 'dp')), parts along dimension 0, may hold values from 1 to 16, 384 in all
- query_lengths: int32 [16], P(('grp', 'dp')), parts along dimension 0, may hold values from 1 to 16, 96 in all
- damping: int32 [1], replicated, may hold values from 3 to 10
Outputs:
- train_grads: bfloat16 [64, 2048], P(('grp', 'dp'), 'tensor'), parts along dimension 0
- query_grads: bfloat16 [16, 2048], P(('grp', 'dp'), 'tensor'), parts along dimension 0
- scores: float32 [64, 8], P(('grp', 'dp')), parts along dimension 0
The draws below stay inside these ranges and needn't reach their ends.
There are 2 independent parts, one for each index of `grp`. The reference program is written for one: setup_inputs(seed, part) draws one part's arguments, and reference() takes and returns one part's arrays. A program takes and returns all parts, laid end to end along the dimension named above; an argument that names none is the same for every part. Nothing has to cross between parts.
Inputs may be any that keep to these rules, and one draw needn't show every extreme that they name: `train_lengths`: each example has 1 to 16 valid tokens, the first ones of its slots; within each part (one corpus shard of 32 examples) the train lengths sum to 384 and some train example of that part has 16; the whole array, all parts end to end, sums to that amount times the number of parts. `query_lengths`: within each part (one corpus shard of 8 examples) the query lengths sum to 96 and some query example of that part has 16; the whole array sums to that amount times the number of parts.
All inputs are finite; a program needn't handle non-finite values.
Results may differ from the reference program's by a relative error of at most 0.0038.
Values may be sent and summed in bfloat16 or wider, within the bound.
A program may use at most 64 MiB of HBM per device.

```python
import math
import jax
import jax.numpy as jnp
import numpy as np
from jax import lax

DIN = 28672
DOUT = 8192
RIN = 64
ROUT = 32
L = 16
N_TR = 32
N_Q = 8


ladder_weights = (20, 13, 10, 8, 7, 6, 5, 5, 4, 4, 4, 3, 3, 3, 3, 3, 2, 2, 2, 2, 2, 2, 2, 2)


def shared_signs(key, shared_code, directions, columns):
    random_bits = jax.random.randint(jax.random.fold_in(key, shared_code), (directions, columns), 0, 2)
    return (2 * random_bits - 1).astype(jnp.float32)


def token_field(key, salt_code, shared_code, row_total, columns, directions):
    signs = shared_signs(key, shared_code, directions, columns)
    levels = jax.random.randint(jax.random.fold_in(key, salt_code), (row_total, directions), -2, 3)
    ladder = jnp.array(ladder_weights[:directions], dtype=jnp.int32)
    coded = (levels * ladder[None, :]).astype(jnp.float32)
    shared = jnp.zeros((row_total, columns), jnp.float32)
    for direction in range(directions):
        shared = shared + coded[:, direction:direction + 1] * signs[direction][None, :]
    shared = shared * 0.03125
    noise_key = jax.random.fold_in(key, salt_code + 1000)
    noise = 0.5 * jax.random.normal(noise_key, (row_total, columns), jnp.float32)
    field = noise + shared
    return jnp.clip(field, -6.0, 6.0).astype(jnp.bfloat16)


def draw_x_train(key, part):
    return token_field(key, 31, 11, N_TR * L, DIN, 24)


def draw_gout_train(key, part):
    return token_field(key, 41, 12, N_TR * L, DOUT, 16)


def draw_x_query(key, part):
    return token_field(key, 51, 11, N_Q * L, DIN, 24)


def draw_gout_query(key, part):
    return token_field(key, 61, 12, N_Q * L, DOUT, 16)


def level_of(own_key, dims, pieces, least, top_value):
    def one(axis_at, shards_of):
        steps = jax.random.uniform(jax.random.fold_in(jax.random.fold_in(own_key, 6), axis_at), (shards_of,), jnp.float32, least / len(pieces), top_value / len(pieces))
        return jnp.repeat(jnp.exp(steps), dims[axis_at] // shards_of).reshape((-1,) + (1,) * (len(dims) - axis_at - 1))

    gain = one(*pieces[0])
    for cut in pieces[1:]:
        gain = gain * one(*cut)
    return gain


def length_profile(amount, total, reach, skew):
    portions = [(1 << 20) // math.isqrt(standing ** skew) + 1 for standing in range(2, amount + 1)]
    rest, given = total - reach - (amount - 1), [1] * (amount - 1)
    while rest > 0:
        candidates = [i for i in range(amount - 1) if given[i] < reach]
        mass, left = sum([portions[i] for i in candidates]), rest
        for i in candidates:
            addition = min(reach - given[i], max(1, left * portions[i] // mass), rest)
            given[i] = given[i] + addition
            rest = rest - addition
    return np.array([reach] + given)


def ragged_sizes(key, number_of, total, reach, slope):
    if number_of == 2:
        one = jax.random.randint(key, (), max(1, total - reach), min(reach, total - 1) + 1)
        return jnp.stack([one, total - one])
    tallies = jnp.asarray(length_profile(number_of, total, reach, slope), jnp.int32)
    twos = (number_of - 1) // 2
    source_of, receiver = tallies[1:1 + 2 * twos:2], tallies[2:2 + 2 * twos:2]
    slack = jnp.minimum(source_of - 1, reach - receiver)
    shifted = jax.random.randint(jax.random.fold_in(key, 1), (twos,), 0, 1 << 20) % (slack + 1)
    tallies = tallies.at[1:1 + 2 * twos:2].set(source_of - shifted).at[2:2 + 2 * twos:2].set(receiver + shifted)
    return tallies[jax.random.permutation(jax.random.fold_in(key, 2), number_of)]


def normal_values(stream_key, dims, width, limit, shards=(), held_as=jnp.bfloat16):
    entries = jax.random.normal(stream_key, dims, jnp.float32) * width
    if len(shards) > 0:
        entries = level_of(stream_key, dims, shards, -0.22, 0.18) * entries
    return jnp.clip(entries, min=-limit, max=limit).astype(held_as)


def setup_inputs(seed: int = 0, part: int = 0) -> dict:
    arg_keys = jax.random.split(jax.random.key(seed), 10)
    part_splits = jax.random.split(jax.random.fold_in(arg_keys[9], part), 10)
    return {
        "x_train": draw_x_train(jax.random.fold_in(jax.random.fold_in(arg_keys[9], part), 71), part),
        "gout_train": draw_gout_train(jax.random.fold_in(jax.random.fold_in(arg_keys[9], part), 71), part),
        "x_query": draw_x_query(jax.random.fold_in(jax.random.fold_in(arg_keys[9], part), 71), part),
        "gout_query": draw_gout_query(jax.random.fold_in(jax.random.fold_in(arg_keys[9], part), 71), part),
        "proj_in": normal_values(arg_keys[4], (DIN, RIN), DIN ** -0.5, 0.03125, ((0, 4),)),
        "proj_out": normal_values(arg_keys[5], (DOUT, ROUT), DOUT ** -0.5, 0.0625, ((0, 4),)),
        "train_lengths": ragged_sizes(part_splits[6], N_TR, N_TR * L * 3 // 4, L, 0).astype(jnp.int32),
        "query_lengths": ragged_sizes(part_splits[7], N_Q, N_Q * L * 3 // 4, L, 0).astype(jnp.int32),
        "damping": jax.random.randint(arg_keys[8], (1,), 3, 11).astype(jnp.int32),
    }


def example_grads(tokens, cotangents, proj_in, proj_out, lengths):
    inner = jnp.dot(tokens.astype(jnp.float32), proj_in.astype(jnp.float32), preferred_element_type=jnp.float32)
    outer = jnp.dot(cotangents.astype(jnp.float32), proj_out.astype(jnp.float32), preferred_element_type=jnp.float32)
    count = lengths.shape[0]
    inner = inner.reshape(count, L, RIN)
    outer = outer.reshape(count, L, ROUT)
    valid = (jnp.arange(L, dtype=jnp.int32)[None, :] < lengths[:, None]).astype(jnp.float32)
    weight = valid / lengths[:, None].astype(jnp.float32)
    summed = jnp.einsum('eti,eto->eio', inner * weight[:, :, None], outer, precision=lax.Precision.HIGHEST)
    return summed.reshape(count, RIN * ROUT).astype(jnp.bfloat16)

def reference(x_train, gout_train, x_query, gout_query, proj_in, proj_out, train_lengths, query_lengths, damping):
    train_grads = example_grads(x_train, gout_train, proj_in, proj_out, train_lengths)
    query_grads = example_grads(x_query, gout_query, proj_in, proj_out, query_lengths)
    kernel = jnp.dot(train_grads.astype(jnp.float32), train_grads.T.astype(jnp.float32), preferred_element_type=jnp.float32)
    cross = jnp.dot(train_grads.astype(jnp.float32), query_grads.T.astype(jnp.float32), preferred_element_type=jnp.float32)
    widened = train_grads.astype(jnp.float32)
    trace = jnp.sum(widened * widened)
    ridge = damping[0].astype(jnp.float32) / 10.0 * trace / N_TR
    system = kernel + ridge * jnp.eye(N_TR, dtype=jnp.float32)
    factor = jnp.linalg.cholesky(system)
    solved = jax.scipy.linalg.cho_solve((factor, True), cross)
    return (train_grads, query_grads, solved * N_TR)
```

```python
import jax
import jax.numpy as jnp
from jax import lax
from jax.experimental import pallas as pl
from jax.experimental.pallas import tpu as pltpu
from jax.sharding import PartitionSpec as P

MESH = pl.DeviceIdType.MESH
F32 = jnp.float32
BF16 = jnp.bfloat16
CHUNKS = 4
NT = (((1,), (1,)), ((), ()))


def weighted_grads(inner, outer, lengths):
    count = lengths.shape[0]
    slots = inner.shape[0] // count
    inner = inner.reshape(count, slots, inner.shape[1])
    outer = outer.reshape(count, slots, outer.shape[1])
    valid = (lax.broadcasted_iota(jnp.int32, (count, slots), 1) < lengths[:, None]).astype(
        jnp.float32
    )
    weight = valid / lengths[:, None].astype(jnp.float32)
    summed = jnp.einsum(
        "eti,eto->eio", inner * weight[:, :, None], outer, precision=lax.Precision.HIGHEST
    )
    return summed.reshape(count, -1).astype(jnp.bfloat16)


def kernel_scores(kernel, cross, scale_code, total_train, first, local_train):
    trace = jnp.trace(kernel)
    ridge = scale_code * trace / total_train
    system = kernel + ridge * jnp.eye(total_train, dtype=jnp.float32)
    factor = jnp.linalg.cholesky(system)
    solved = jax.scipy.linalg.cho_solve((factor, True), cross)
    picked = lax.dynamic_slice_in_dim(solved, first, local_train, 0)
    return picked * total_train


def iota(shape, dim):
    return lax.broadcasted_iota(jnp.int32, shape, dim)


def fused_kernel(
    xt_hbm, gt_hbm, xq_hbm, gq_hbm, pi_hbm, po_hbm, tlen, qlen, damp,
    tg_ref, qg_ref, sc_ref,
    xt, gt, xq, gq, pi, po,
    outer_send, outer_recv, inner_send, inner_recv, grads, gram_send, gram_recv,
    load_sem, send_sem, recv_sem,
):
    dp, tp = lax.axis_index("dp"), lax.axis_index("tensor")
    barrier = pltpu.get_barrier_semaphore()
    for d in range(1, 4):
        for axis, me in (("tensor", tp), ("dp", dp)):
            pl.semaphore_signal(
                barrier, inc=1, device_id={axis: lax.rem(me + d, 4)}, device_id_type=MESH
            )
    loads = []
    for src, dst in ((gt_hbm, gt), (gq_hbm, gq), (po_hbm, po)):
        loads.append(pltpu.make_async_copy(src, dst, load_sem.at[len(loads)]))
    width = xt.shape[1] // CHUNKS
    for c in range(CHUNKS):
        cols = pl.ds(c * width, width)
        for src, dst in ((xt_hbm, xt), (xq_hbm, xq), (pi_hbm, pi)):
            loads.append(
                pltpu.make_async_copy(src.at[:, cols], dst.at[:, cols], load_sem.at[len(loads)])
            )
    for load in loads:
        load.start()

    lane8 = iota((8, 128), 1)
    row8 = iota((8, 128), 0)
    block32 = lane8 >> 5
    lane = iota((8, 256), 1)
    length = jnp.ones((8, 256), jnp.int32)
    for e in range(8):
        length = jnp.where((lane >> 4) == e, tlen[e], length)
    for e in range(2):
        length = jnp.where((lane >> 4) == 8 + e, qlen[e], length)
    weight = jnp.where(
        ((lane & 15) < length) & (lane < 160), 1.0 / length.astype(F32), 0.0
    )
    pick_row, pick_lane = iota((16, 256), 0), iota((16, 256), 1)
    picks = jnp.where((pick_lane >> 4) == pick_row, 1.0, 0.0).astype(BF16)

    def copy(index, src, dst, axis, me, d):
        return pltpu.make_async_remote_copy(
            src_ref=src, dst_ref=dst, send_sem=send_sem.at[index], recv_sem=recv_sem.at[index],
            device_id={axis: lax.rem(me + d, 4)}, device_id_type=MESH,
        )

    for load in loads[:3]:
        load.wait()
    gqv = gq[...]
    outer = lax.dot_general(
        po[...], jnp.concatenate([gt[...], gqv, gqv, gqv, gqv], axis=0), NT,
        preferred_element_type=F32,
    )
    packed = jnp.zeros((8, 128), F32)
    for g in range(4):
        packed = jnp.where(block32 == g, outer[8 * g:8 * g + 8, 128:], packed)
    outer_send[0:32, :] = outer[:, :128]
    outer_send[32:40, :] = packed
    pl.semaphore_wait(barrier, 6)
    copies = []
    outer_copies = [
        copy(d - 1, outer_send, outer_recv.at[d - 1], "tensor", tp, d) for d in (1, 2, 3)
    ]
    for item in outer_copies:
        item.start()

    inner = jnp.zeros((64, 256), F32)
    for c in range(CHUNKS):
        for load in loads[3 + 3 * c:6 + 3 * c]:
            load.wait()
        cols = pl.ds(c * width, width)
        xqv = xq[:, cols]
        inner = inner + lax.dot_general(
            pi[:, cols], jnp.concatenate([xt[:, cols], xqv, xqv, xqv, xqv], axis=0), NT,
            preferred_element_type=F32,
        )
    for d in range(4):
        inner_send[d, 0:16, :] = inner[16 * d:16 * d + 16, :128]
        first = inner[16 * d:16 * d + 8, 128:]
        inner_send[d, 16:24, :] = jnp.where(
            block32 == 1, inner[16 * d + 8:16 * d + 16, 128:], first
        )
    inner_copies = [
        copy(2 + d, inner_send.at[lax.rem(tp + d, 4)], inner_recv.at[d - 1], "tensor", tp, d)
        for d in (1, 2, 3)
    ]
    for item in inner_copies:
        item.start()

    for item in outer_copies:
        item.wait_recv()
    total = outer_send[...] + outer_recv[0] + outer_recv[1] + outer_recv[2]
    query = total[32:40, :]
    outer_t = jnp.concatenate(
        [
            jnp.concatenate(
                [total[8 * g:8 * g + 8], query if g == 0 else pltpu.roll(query, 128 - 32 * g, 1)],
                axis=1,
            )
            * weight
            for g in range(4)
        ],
        axis=0,
    )
    own = inner_send[tp]
    for item in inner_copies:
        item.wait_recv()
    total = own + inner_recv[0] + inner_recv[1] + inner_recv[2]
    query = total[16:24, :]
    inner_t = jnp.concatenate(
        [
            total[0:16, :],
            jnp.concatenate([query, pltpu.roll(query, 96, 1)], axis=0),
        ],
        axis=1,
    )
    product = jnp.concatenate(
        [jnp.broadcast_to(inner_t[i:i + 1, :], (32, 256)) * outer_t for i in range(16)], axis=0
    )
    high = product.astype(BF16)
    rest = product - high.astype(F32)
    middle = rest.astype(BF16)
    low = (rest - middle.astype(F32)).astype(BF16)
    summed = (
        lax.dot_general(picks, high, NT, preferred_element_type=F32)
        + lax.dot_general(picks, middle, NT, preferred_element_type=F32)
        + lax.dot_general(picks, low, NT, preferred_element_type=F32)
    )
    train_grads = summed[0:8, :]
    query_grads = summed[8:16, :]
    packed = query_grads[:, 0:128]
    for c in range(1, 4):
        packed = packed + pltpu.roll(query_grads[:, 128 * c:128 * c + 128], 2 * c, 0)
    grads[dp] = jnp.concatenate([train_grads, packed], axis=1).astype(BF16)
    grad_copies = [copy(5 + d, grads.at[dp], grads.at[dp], "dp", dp, d) for d in (1, 2, 3)]
    for item in grad_copies:
        item.start()
    tg_ref[...] = train_grads.astype(BF16)
    qg_ref[...] = query_grads[0:2, :].astype(BF16)
    for item in grad_copies:
        item.wait_recv()

    blocks = [grads[s].astype(F32) for s in range(4)]
    rows = jnp.concatenate([block[:, :512] for block in blocks], axis=0)
    pieces = []
    for c in range(4):
        piece = jnp.zeros((8, 128), F32)
        for s in range(4):
            turned = blocks[s][:, 512:]
            if (2 * s - 2 * c) % 8:
                turned = pltpu.roll(turned, (2 * s - 2 * c) % 8, 0)
            piece = jnp.where((row8 >> 1) == s, turned, piece)
        pieces.append(piece)
    queries = jnp.concatenate(pieces, axis=1)
    rows16 = rows.astype(BF16)
    right = jnp.concatenate([rows16] * 4 + [jnp.concatenate([queries] * 16, axis=0).astype(BF16)], axis=0)
    gram = lax.dot_general(rows16, right, NT, preferred_element_type=F32)
    trace = jnp.sum(rows * rows, axis=(0, 1), keepdims=True)
    system, cross = gram[0:8, :128], jnp.where(lane8 < 8, gram[0:8, 128:], trace)
    for g in range(1, 4):
        system = jnp.where(block32 == g, gram[8 * g:8 * g + 8, :128], system)
        cross = jnp.where((lane8 >> 3) == g, gram[8 * g:8 * g + 8, 128:], cross)
    gram_send[0:8, :] = system
    gram_send[8:16, :] = cross
    gram_copies = [
        copy(8 + d, gram_send, gram_recv.at[d - 1], "tensor", tp, d) for d in (1, 2, 3)
    ]
    for item in gram_copies:
        item.start()
    for item in gram_copies:
        item.wait_recv()
    total = gram_send[...] + gram_recv[0] + gram_recv[1] + gram_recv[2]
    system, cross = total[0:8], total[8:16]
    ridge = jnp.broadcast_to(cross[:, 127:128], (8, 128)) * (damp[0].astype(F32) / 10.0) / 32.0
    columns = []
    for j in range(32):
        column = [
            jnp.broadcast_to(system[:, 32 * g + j:32 * g + j + 1], (8, 128)) for g in range(4)
        ]
        g, r = j // 8, j % 8
        column[g] = jnp.where(row8 == r, column[g] + ridge, column[g])
        columns.append(column)
    right = [cross if g == 0 else pltpu.roll(cross, 128 - 8 * g, 1) for g in range(4)]
    inverse = [jnp.zeros((8, 128), F32)] * 4
    for k in range(32):
        g0, r0 = k // 8, k % 8
        column = columns[k]
        reciprocal = 1.0 / jnp.broadcast_to(column[g0][r0:r0 + 1, :], (8, 128))
        here = row8 == r0
        inverse[g0] = jnp.where(here, reciprocal, inverse[g0])
        factor = [column[g] * reciprocal for g in range(4)]
        factor[g0] = jnp.where(here, 0.0, factor[g0])
        for other in columns[k + 1:] + [right]:
            pivot = jnp.broadcast_to(other[g0][r0:r0 + 1, :], (8, 128))
            for g in range(4):
                other[g] = other[g] - factor[g] * pivot
    answer = right[0] * inverse[0]
    for g in range(1, 4):
        answer = jnp.where(dp == g, right[g] * inverse[g], answer)
    sc_ref[...] = (answer * 32.0)[:, :8]
    for item in outer_copies + inner_copies + grad_copies + gram_copies:
        item.wait_send()


def fused(x_train, gout_train, x_query, gout_query, proj_in, proj_out, train_lengths, query_lengths, damping):
    any_spec = pl.BlockSpec(memory_space=pl.ANY)
    smem = pl.BlockSpec(memory_space=pltpu.SMEM)
    vmem = pl.BlockSpec(memory_space=pltpu.VMEM)
    pi, po = proj_in.T, proj_out.T
    big = [pltpu.VMEM(a.shape, BF16) for a in (x_train, gout_train, x_query, gout_query, pi, po)]
    return pl.pallas_call(
        fused_kernel,
        out_shape=(
            jax.ShapeDtypeStruct((8, 512), BF16),
            jax.ShapeDtypeStruct((2, 512), BF16),
            jax.ShapeDtypeStruct((8, 8), F32),
        ),
        in_specs=[any_spec] * 6 + [smem] * 3,
        out_specs=(vmem, vmem, vmem),
        scratch_shapes=big
        + [
            pltpu.VMEM((40, 128), F32),
            pltpu.VMEM((3, 40, 128), F32),
            pltpu.VMEM((4, 24, 128), F32),
            pltpu.VMEM((3, 24, 128), F32),
            pltpu.VMEM((4, 8, 640), BF16),
            pltpu.VMEM((16, 128), F32),
            pltpu.VMEM((3, 16, 128), F32),
            pltpu.SemaphoreType.DMA((3 + 3 * CHUNKS,)),
            pltpu.SemaphoreType.DMA((12,)),
            pltpu.SemaphoreType.DMA((12,)),
        ],
        compiler_params=pltpu.CompilerParams(collective_id=0, has_side_effects=True),
    )(x_train, gout_train, x_query, gout_query, pi, po, train_lengths, query_lengths, damping)


def fits(x_train, gout_train, proj_in, proj_out, train_lengths, query_lengths):
    return (
        lax.axis_size("dp") == 4
        and lax.axis_size("tensor") == 4
        and train_lengths.shape[0] == 8
        and query_lengths.shape[0] == 2
        and x_train.shape[0] == 128
        and proj_in.shape[1] == 64
        and proj_out.shape[1] == 32
        and x_train.shape[1] % (128 * CHUNKS) == 0
        and gout_train.shape[1] % 128 == 0
    )


def shards(
    x_train,
    gout_train,
    x_query,
    gout_query,
    proj_in,
    proj_out,
    train_lengths,
    query_lengths,
    damping,
):
    if fits(x_train, gout_train, proj_in, proj_out, train_lengths, query_lengths):
        return fused(
            x_train, gout_train, x_query, gout_query, proj_in, proj_out,
            train_lengths, query_lengths, damping,
        )
    local_train = train_lengths.shape[0]
    total_train = local_train * lax.axis_size("dp")
    first = lax.axis_index("dp") * local_train
    scale_code = damping[0].astype(jnp.float32) / 10.0
    train_inner = jnp.dot(x_train, proj_in, preferred_element_type=jnp.float32)
    query_inner = jnp.dot(x_query, proj_in, preferred_element_type=jnp.float32)
    train_outer = jnp.dot(gout_train, proj_out, preferred_element_type=jnp.float32)
    query_outer = jnp.dot(gout_query, proj_out, preferred_element_type=jnp.float32)
    summed = lax.psum((train_inner, query_inner, train_outer, query_outer), "tensor")
    train_full = weighted_grads(summed[0], summed[2], train_lengths)
    query_full = weighted_grads(summed[1], summed[3], query_lengths)
    share = train_full.shape[1] // lax.axis_size("tensor")
    offset = lax.axis_index("tensor") * share
    train_grads = lax.dynamic_slice_in_dim(train_full, offset, share, 1)
    query_grads = lax.dynamic_slice_in_dim(query_full, offset, share, 1)
    all_train, all_query = (
        lax.all_gather(train_full, "dp", axis=0, tiled=True),
        lax.all_gather(query_full, "dp", axis=0, tiled=True),
    )
    kernel = jnp.dot(all_train, all_train.T, preferred_element_type=jnp.float32)
    cross = jnp.dot(all_train, all_query.T, preferred_element_type=jnp.float32)
    scores = kernel_scores(kernel, cross, scale_code, total_train, first, local_train)
    return (train_grads, query_grads, scores)


def solution(mesh):
    placed = (
        P(("grp", "dp"), "tensor"),
        P(("grp", "dp"), "tensor"),
        P(("grp", "dp"), "tensor"),
        P(("grp", "dp"), "tensor"),
        P("tensor", None),
        P("tensor", None),
        P(("grp", "dp")),
        P(("grp", "dp")),
        P(),
    )
    return jax.shard_map(
        shards,
        mesh=mesh,
        in_specs=placed,
        out_specs=(P(("grp", "dp"), "tensor"), P(("grp", "dp"), "tensor"), P(("grp", "dp"), None)),
        check_vma=False,
    )
```
